256 devices in a mesh: seg: 4 (over x), pair: 64 (over z, y, core).
Axes of the slice: x: 4, y: 4, z: 8, core: 2. Of those that a mesh axis runs over, the one named last changes fastest.
Arguments:
- traces: bfloat16 [4, 4096, 640], P('seg', 'pair'), may hold values from -160 to 160
- station_slot: int32 [64, 64], P('pair'), may hold values from 0 to 63, each once within a row
- block_pairs: int32 [256, 2], P('pair'), may hold values from 0 to 127, as said below
- pair_count: int32 [64], P('pair'), may hold values from 2 to 4
Outputs:
- correlations: bfloat16 [256, 1281, 1024], P('pair', None, 'seg')
The draws below stay inside these ranges and needn't reach their ends.
Inputs may be any that keep to these rules, and one draw needn't show every extreme that they name: `block_pairs`: rows 4 o to 4 o + 3 belong to owner o. The first block of each row is one of o's own blocks 2 o to 2 o + 1; the second differs from the first and lies on device o - 1, o or o + 1; of the blocks of device o - 1, and of those of device o + 1, at most one is named in owner o's rows; the first row of each owner names a block of o - 1 and the second a block of o + 1 where those devices exist.
All inputs are finite; a program needn't handle non-finite values.
Results may differ from the reference program's by a relative error of at most 0.012.
The reference program's roundings to bfloat16 on the way count: a program that leaves them out, or rounds other values in their place, can miss the bound.
Values may be sent and summed in bfloat16 or wider, within the bound.
No kernel may reach another device: no remote copies, remote signals or barrier semaphores. Data moves between devices by JAX's collectives and lax.ppermute only.
A program may use at most 128 MiB of HBM per device.

```python
import math
import jax
import jax.numpy as jnp
from jax import lax

SAMPLES = 640
HALF_BAND = 64
BLK = 32
BPD = 2
SLOTS = 4
STA_DEV = 64
STATIONS = 4096
NB = 128
SEG = 4
PAIRS = 256
N_PAIR = 64


def draw_traces(key, part):
    subkeys = jax.random.split(key, 5)
    shape = (SEG, STATIONS, SAMPLES)
    noise = jnp.clip(jax.random.normal(subkeys[0], shape, jnp.float32), -6.0, 6.0)
    gains = jnp.exp(jax.random.uniform(subkeys[1], (1, STATIONS, 1), jnp.float32, 0.0, math.log(10.0)))
    timeline = jnp.arange(SAMPLES, dtype=jnp.float32)[None, None, :]
    frequencies = jax.random.uniform(subkeys[2], (3, 1, STATIONS, 1), jnp.float32, 0.02, 0.48)
    amplitudes = jnp.exp(jax.random.uniform(subkeys[3], (3, 1, STATIONS, 1), jnp.float32, 0.0, math.log(8.0)))
    phases = jax.random.uniform(subkeys[4], (3, SEG, STATIONS, 1), jnp.float32, 0.0, 2.0 * math.pi)
    lines = jnp.zeros(shape, jnp.float32)
    for term_index in range(3):
        lines = lines + amplitudes[term_index] * jnp.sin(2.0 * math.pi * frequencies[term_index] * timeline + phases[term_index])
    return (gains * (noise + lines) / 3.0).astype(jnp.bfloat16)


def draw_block_pairs(key, part):
    subkeys = jax.random.split(key, 5)
    owners = jnp.arange(N_PAIR, dtype=jnp.int32)[:, None]
    first_pick = jax.random.randint(subkeys[0], (N_PAIR, SLOTS), 0, BPD, dtype=jnp.int32)
    first_block = BPD * owners + first_pick
    offset = jax.random.randint(subkeys[1], (N_PAIR, SLOTS), 1, BPD, dtype=jnp.int32)
    other_block = BPD * owners + jnp.mod(first_pick + offset, BPD)
    left_block = BPD * (owners - 1) + jax.random.randint(subkeys[2], (N_PAIR, 1), 0, BPD, dtype=jnp.int32)
    right_block = BPD * (owners + 1) + jax.random.randint(subkeys[3], (N_PAIR, 1), 0, BPD, dtype=jnp.int32)
    link_kind = jax.random.randint(subkeys[4], (N_PAIR, SLOTS), 0, 3, dtype=jnp.int32)
    slot_index = jnp.arange(SLOTS, dtype=jnp.int32)[None, :]
    link_kind = jnp.where(slot_index == 0, 0, jnp.where(slot_index == 1, 1, link_kind))
    left_exists = owners > 0
    right_exists = owners < N_PAIR - 1
    second_block = jnp.where((link_kind == 0) & left_exists, left_block, jnp.where((link_kind == 1) & right_exists, right_block, other_block))
    return jnp.stack([first_block, second_block], axis=2).reshape(N_PAIR * SLOTS, 2).astype(jnp.int32)


def draw_pair_count(key, part):
    subkeys = jax.random.split(key, 2)
    counts = jax.random.randint(subkeys[0], (N_PAIR,), 2, SLOTS + 1, dtype=jnp.int32)
    busiest = jax.random.randint(subkeys[1], (), 0, N_PAIR, dtype=jnp.int32)
    return jnp.where(jnp.arange(N_PAIR, dtype=jnp.int32) == busiest, SLOTS, counts).astype(jnp.int32)


def setup_inputs(seed: int = 0) -> dict:
    arg_keys = jax.random.split(jax.random.key(seed), 5)
    traces = draw_traces(jax.random.fold_in(arg_keys[4], 71), 0)
    station_slot = jax.vmap(lambda own: jax.random.permutation(own, STA_DEV))(jax.random.split(arg_keys[1], N_PAIR)).reshape((N_PAIR, STA_DEV)).astype(jnp.int32)
    block_pairs = draw_block_pairs(jax.random.fold_in(arg_keys[4], 71), 0)
    pair_count = draw_pair_count(jax.random.fold_in(arg_keys[4], 71), 0)
    return dict(traces=traces, station_slot=station_slot, block_pairs=block_pairs, pair_count=pair_count)


def forward_table(samples):
    sample_index = jnp.arange(samples, dtype=jnp.int32)
    phase_index = jnp.mod(sample_index[:, None] * sample_index[None, :], 2 * samples)
    angles = phase_index.astype(jnp.float32) * (math.pi / samples)
    return jnp.concatenate([jnp.cos(angles).astype(jnp.bfloat16), (-jnp.sin(angles)).astype(jnp.bfloat16)], axis=1)

def inverse_table(samples):
    freq_bins = jnp.arange(samples, dtype=jnp.int32)
    shifts = jnp.arange(2 * samples + 1, dtype=jnp.int32) - samples
    phase_index = jnp.mod(shifts[:, None] * freq_bins[None, :], 2 * samples)
    angles = phase_index.astype(jnp.float32) * (math.pi / samples)
    weight = jnp.where(freq_bins == 0, 1.0, 2.0).astype(jnp.float32)[None, :]
    return jnp.concatenate([(weight * jnp.cos(angles)).astype(jnp.bfloat16), (-weight * jnp.sin(angles)).astype(jnp.bfloat16)], axis=1)

def whiten(series, half_band):
    samples = series.shape[1]
    spectra = jnp.dot(series, forward_table(samples), preferred_element_type=jnp.float32)
    real_part = spectra[:, :samples]
    imag_part = spectra[:, samples:]
    powers = real_part * real_part + imag_part * imag_part
    freq_bins = jnp.arange(samples, dtype=jnp.int32)
    window = (jnp.abs(freq_bins[:, None] - freq_bins[None, :]) <= half_band).astype(jnp.float32)
    counts = lax.optimization_barrier(jnp.sum(window, axis=0))
    smooth = jnp.dot(powers, window, precision=lax.Precision.HIGHEST) / counts[None, :]
    factor = lax.rsqrt(smooth + 1e-06)
    return (spectra * jnp.concatenate([factor, factor], axis=1)).astype(jnp.bfloat16)

def cross_spectra(first_rows, second_rows):
    bin_count = first_rows.shape[2] // 2
    first_real = first_rows[..., :bin_count]
    first_imag = first_rows[..., bin_count:]
    second_real = second_rows[..., :bin_count]
    second_imag = second_rows[..., bin_count:]

    def product(left_part, right_part):
        return jnp.einsum('sif,sjf->fij', left_part, right_part, precision=lax.Precision.HIGHEST)
    real_sum = product(first_real, second_real) + product(first_imag, second_imag)
    imag_sum = product(first_imag, second_real) - product(first_real, second_imag)
    return jnp.concatenate([real_sum.reshape(bin_count, -1), imag_sum.reshape(bin_count, -1)], axis=0)

def reference(traces, station_slot, block_pairs, pair_count):
    white = whiten(traces.reshape(SEG * STATIONS, SAMPLES), HALF_BAND)
    white = lax.optimization_barrier(white).reshape(SEG, STATIONS, 2 * SAMPLES)
    position = (jnp.arange(N_PAIR, dtype=jnp.int32)[:, None] * STA_DEV + station_slot).reshape(STATIONS)
    ordered = jnp.zeros_like(white).at[:, position, :].set(white)
    blocks = ordered.reshape(SEG, NB, BLK, 2 * SAMPLES)
    inverse = lax.optimization_barrier(inverse_table(SAMPLES)).astype(jnp.float32)
    norm_scale = 1.0 / math.sqrt(2.0 * SAMPLES * SEG)
    live_mask = (jnp.arange(SLOTS, dtype=jnp.int32)[None, :] < pair_count[:, None]).reshape(PAIRS)

    def correlate(inputs):
        pair_row, is_live = inputs
        first_rows = jnp.take(blocks, pair_row[0], axis=1).astype(jnp.float32)
        second_rows = jnp.take(blocks, pair_row[1], axis=1).astype(jnp.float32)
        stacked = cross_spectra(first_rows, second_rows)
        stacked = lax.optimization_barrier(stacked.astype(jnp.bfloat16)).astype(jnp.float32)
        correlated = jnp.dot(inverse, stacked, precision=lax.Precision.HIGHEST) * norm_scale
        return jnp.where(is_live, correlated, 0.0).astype(jnp.bfloat16)
    return lax.map(correlate, (block_pairs, live_mask))
```

```python
import functools
import math

import jax
import jax.numpy as jnp
import numpy as np
from jax import lax
from jax.experimental import pallas as pl
from jax.experimental.pallas import tpu as pltpu
from jax.sharding import Mesh
from jax.sharding import PartitionSpec as P

N = 640
HALF_BAND = 64
BLK = 32
SEG = 4
SLOTS = 4
LANES = 128
KB = N // LANES
ROWS = SEG * BLK
OUT_ROWS = (2 * N + 1) * 8
NT = (((1,), (1,)), ((), ()))
VMEM = pl.BlockSpec(memory_space=pltpu.VMEM)
SMEM = pl.BlockSpec(memory_space=pltpu.SMEM)
f32 = jnp.float32
bf16 = jnp.bfloat16


def bin_order():
    return np.concatenate([np.arange(0, N, 2), np.arange(1, N, 2)])


def fourier_table():
    bins = bin_order()
    phase = (np.arange(N)[:, None] * bins[None, :]) % (2 * N)
    angle = phase * (math.pi / N)
    real = np.cos(angle).reshape(N, KB, 1, LANES)
    imag = -np.sin(angle).reshape(N, KB, 1, LANES)
    return np.concatenate([real, imag], axis=2).reshape(N, 2 * N).astype(bf16)


def window_table():
    bins = bin_order()
    return (np.abs(bins[:, None] - bins[None, :]) <= HALF_BAND).astype(bf16)


def bin_rows():
    bins = bin_order()
    counts = np.minimum(bins, HALF_BAND) + np.minimum(N - 1 - bins, HALF_BAND) + 1
    weight = np.where(bins == 0, 0.5, 1.0)
    return np.stack([1.0 / counts, weight]).astype(np.float32)


def order_kernel(slot_ref, gathered_ref, blocks_ref):
    place = lax.broadcasted_iota(jnp.int32, (2 * BLK, 2 * BLK), 0)
    onehot = (place == slot_ref[...]).astype(bf16)
    for s in range(SEG):
        rows = jnp.dot(onehot, gathered_ref[s], preferred_element_type=f32).astype(bf16)
        blocks_ref[0, s * BLK : (s + 1) * BLK, :] = rows[:BLK]
        blocks_ref[1, s * BLK : (s + 1) * BLK, :] = rows[BLK:]


def order_rows(station_slot, gathered):
    return pl.pallas_call(
        order_kernel,
        out_shape=jax.ShapeDtypeStruct((2, ROWS, N), bf16),
        in_specs=[VMEM, VMEM],
        out_specs=VMEM,
        name="order_rows",
    )(station_slot, gathered)


def whiten_rows(rows, table_ref, window_ref, bins_ref, spec_ref, hi_ref, lo_ref, store):
    for kb in range(KB):
        cols = slice(2 * kb * LANES, 2 * (kb + 1) * LANES)
        lanes = slice(kb * LANES, (kb + 1) * LANES)
        spec = jnp.dot(rows, table_ref[:, cols], preferred_element_type=f32)
        spec_ref[:, cols] = spec
        real, imag = spec[:, :LANES], spec[:, LANES:]
        power = real * real + imag * imag
        high = power.astype(bf16)
        hi_ref[:, lanes] = high
        lo_ref[:, lanes] = (power - high.astype(f32)).astype(bf16)
    total = jnp.dot(hi_ref[...], window_ref[...], preferred_element_type=f32)
    total += jnp.dot(lo_ref[...], window_ref[...], preferred_element_type=f32)
    factor = lax.rsqrt(total * bins_ref[0:1, :] + 1e-06)
    for kb in range(KB):
        scale = factor[:, kb * LANES : (kb + 1) * LANES]
        for part in range(2):
            start = (2 * kb + part) * LANES
            cols = slice(start, start + LANES)
            store(cols, (spec_ref[:, cols] * scale).astype(bf16))


def own_kernel(blocks_ref, table_ref, window_ref, bins_ref, white_ref, spec_ref, hi_ref, lo_ref):
    rows = blocks_ref[...].reshape(2 * ROWS, N)

    def store(cols, value):
        white_ref[:, cols] = value.astype(f32)

    whiten_rows(rows, table_ref, window_ref, bins_ref, spec_ref, hi_ref, lo_ref, store)


def whiten_scratch():
    return [
        pltpu.VMEM((2 * ROWS, 2 * N), f32),
        pltpu.VMEM((2 * ROWS, N), bf16),
        pltpu.VMEM((2 * ROWS, N), bf16),
    ]


def whiten_own(blocks, table, window, bins):
    return pl.pallas_call(
        own_kernel,
        out_shape=jax.ShapeDtypeStruct((2 * ROWS, 2 * N), f32),
        in_specs=[VMEM] * 4,
        out_specs=VMEM,
        scratch_shapes=whiten_scratch(),
        name="whiten_own",
    )(blocks, table, window, bins)


def main_kernel(
    meta_ref,
    own_ref,
    mate_ref,
    far_ref,
    table_ref,
    window_ref,
    bins_ref,
    out_ref,
    white_ref,
    spec_ref,
    hi_ref,
    lo_ref,
    mid_ref,
    first_ref,
    cross_ref,
    lag_ref,
    low_ref,
    sems,
):
    owner, seg_index, count = meta_ref[9], meta_ref[10], meta_ref[8]
    mate = owner + 1 - 2 * (owner % 2)

    mate_pick, far_pick = 0, 0
    first_base, second_base = [], []
    for z in range(SLOTS):
        first, second = meta_ref[2 * z], meta_ref[2 * z + 1]
        device, half = second // 2, second % 2
        is_own, is_mate = device == owner, device == mate
        mate_pick = jnp.where(is_mate, half, mate_pick)
        far_pick = jnp.where(is_own | is_mate, far_pick, half)
        place = jnp.where(is_own, half, jnp.where(is_mate, 2, 3))
        second_base.append(place * ROWS)
        first_base.append((first % 2) * ROWS + seg_index * (BLK // SEG))

    white_ref[: 2 * ROWS, :] = own_ref[...]
    rows = jnp.concatenate([mate_ref[mate_pick], far_ref[far_pick]], axis=0)

    def store(cols, value):
        white_ref[2 * ROWS :, cols] = value.astype(f32)

    whiten_rows(rows, table_ref, window_ref, bins_ref, spec_ref, hi_ref, lo_ref, store)

    middle = table_ref[:, 2 * 2 * LANES : 2 * 3 * LANES]
    even = lax.broadcasted_iota(jnp.int32, (1, 2 * LANES), 1) % LANES < LANES // 2
    mid_ref[:, : 2 * LANES] = jnp.where(even, middle, jnp.zeros_like(middle))
    mid_ref[:, 2 * LANES :] = jnp.where(even, jnp.zeros_like(middle), middle)

    for z in range(SLOTS):
        for s in range(SEG):
            start = pl.multiple_of(first_base[z] + s * BLK, 8)
            first_ref[s * 8 : (s + 1) * 8, :] = white_ref[pl.ds(start, 8), :]

        def cross_step(kb, carry, z=z):
            real_col = pl.multiple_of(2 * kb * LANES, LANES)
            imag_col = pl.multiple_of((2 * kb + 1) * LANES, LANES)
            weight = bins_ref[1:2, pl.ds(pl.multiple_of(kb * LANES, LANES), LANES)]
            for half in range(2):
                second = []
                for s in range(SEG):
                    start = pl.multiple_of(second_base[z] + s * BLK + half * 16, 16)
                    second.append(
                        (
                            white_ref[pl.ds(start, 16), pl.ds(real_col, LANES)] * weight,
                            white_ref[pl.ds(start, 16), pl.ds(imag_col, LANES)] * weight,
                        )
                    )
                for i in range(BLK // SEG):
                    real, imag = 0.0, 0.0
                    for s in range(SEG):
                        row = slice(s * 8 + i, s * 8 + i + 1)
                        a_re = first_ref[row, pl.ds(real_col, LANES)]
                        a_im = first_ref[row, pl.ds(imag_col, LANES)]
                        b_re, b_im = second[s]
                        real = real + (a_re * b_re + a_im * b_im)
                        imag = imag + (a_im * b_re - a_re * b_im)
                    at = slice(i * BLK + half * 16, i * BLK + half * 16 + 16)
                    cross_ref[at, pl.ds(real_col, LANES)] = real.astype(bf16)
                    cross_ref[at, pl.ds(imag_col, LANES)] = imag.astype(bf16)
            return carry

        lax.fori_loop(0, KB, cross_step, 0)

        step = N // 2
        for half in range(2):
            at = slice(half * step, (half + 1) * step)
            low_side = lax.dot_general(
                table_ref[at, : 4 * LANES], cross_ref[:, : 4 * LANES], NT, preferred_element_type=f32
            ) + lax.dot_general(
                mid_ref[at, : 2 * LANES],
                cross_ref[:, 4 * LANES : 6 * LANES],
                NT,
                preferred_element_type=f32,
            )
            high_side = lax.dot_general(
                table_ref[at, 6 * LANES :], cross_ref[:, 6 * LANES :], NT, preferred_element_type=f32
            ) + lax.dot_general(
                mid_ref[at, 2 * LANES :],
                cross_ref[:, 4 * LANES : 6 * LANES],
                NT,
                preferred_element_type=f32,
            )
            minus, plus = low_side - high_side, low_side + high_side
            for ct in range(2):
                lanes = slice(ct * LANES, (ct + 1) * LANES)
                start = half * step * 8 + ct * 4 + z
                lag_ref[pl.ds(start, step, stride=8), :] = minus[:, lanes]
                lag_ref[pl.ds(start + N * 8, step, stride=8), :] = plus[:, lanes]

    slot = lax.broadcasted_iota(jnp.int32, (8, LANES), 0) % SLOTS
    scale = 2.0 / math.sqrt(2.0 * N * SEG)
    chunks = 8
    size = 2 * N * 8 // chunks
    copies = []
    for c in range(chunks):
        value = lag_ref[c * size : (c + 1) * size, :].reshape(size // 8, 8, LANES)
        value = jnp.where((slot < count)[None], value * scale, 0.0)
        low_ref[c * size : (c + 1) * size, :] = value.reshape(size, LANES).astype(bf16)
        copy = pltpu.make_async_copy(
            low_ref.at[pl.ds(c * size, size)], out_ref.at[pl.ds(c * size, size)], sems.at[c]
        )
        copy.start()
        copies.append(copy)
    last = pltpu.make_async_copy(
        low_ref.at[pl.ds(0, 8)], out_ref.at[pl.ds(2 * N * 8, 8)], sems.at[chunks]
    )
    last.start()
    for copy in copies:
        copy.wait()
    last.wait()


def correlate(meta, own_white, mate, far, table, window, bins):
    return pl.pallas_call(
        main_kernel,
        out_shape=jax.ShapeDtypeStruct((OUT_ROWS, LANES), bf16),
        in_specs=[SMEM] + [VMEM] * 6,
        out_specs=pl.BlockSpec(memory_space=pltpu.HBM),
        scratch_shapes=[pltpu.VMEM((4 * ROWS, 2 * N), f32)]
        + whiten_scratch()
        + [
            pltpu.VMEM((N, 4 * LANES), bf16),
            pltpu.VMEM((BLK, 2 * N), f32),
            pltpu.VMEM((2 * ROWS, 2 * N), bf16),
            pltpu.VMEM((2 * N * 8, LANES), f32),
            pltpu.VMEM((2 * N * 8, LANES), bf16),
            pltpu.SemaphoreType.DMA((9,)),
        ],
        name="correlate",
    )(meta, own_white, mate, far, table, window, bins)


def unpack(packed):
    lags = 2 * N + 1
    split = packed.reshape(lags, 2, SLOTS, LANES)
    return jnp.transpose(split, (2, 0, 1, 3)).reshape(SLOTS, lags, 2 * LANES)


def body(traces, station_slot, block_pairs, pair_count):
    pair = ("chip", "core")
    owners = lax.axis_size("chip") * 2
    table = jnp.asarray(fourier_table())
    window = jnp.asarray(window_table())
    bins = jnp.asarray(bin_rows())

    def along(distance):
        return [(i, (i + distance) % SEG) for i in range(SEG)]

    gathered = jnp.concatenate(
        [traces] + [lax.ppermute(traces, "seg", along(d)) for d in (1, 3, 2)], axis=0
    )
    blocks = order_rows(station_slot, gathered)
    mates = [(i, i ^ 1) for i in range(owners)]
    crossing = [(i, i + 1) for i in range(1, owners - 1, 2)]
    crossing += [(b, a) for a, b in crossing]
    far = lax.ppermute(blocks, pair, crossing)
    mate = lax.ppermute(blocks, pair, mates)
    own_white = whiten_own(blocks, table, window, bins)
    place = jnp.stack([lax.axis_index(pair), lax.axis_index("seg")]).astype(jnp.int32)
    meta = jnp.concatenate([block_pairs.reshape(-1), pair_count, place])
    return unpack(correlate(meta, own_white, mate, far, table, window, bins))


def solution(mesh):
    devices = mesh.devices.reshape(SEG, -1, 2)
    split = Mesh(devices, ("seg", "chip", "core"))
    pair = ("chip", "core")
    return jax.shard_map(
        body,
        mesh=split,
        in_specs=(P("seg", pair, None), P(pair, None), P(pair, None), P(pair)),
        out_specs=P(pair, None, "seg"),
        check_vma=False,
    )
```

```python
import functools
import math

import jax
import jax.numpy as jnp
import numpy as np
from jax import lax
from jax.experimental import pallas as pl
from jax.experimental.pallas import tpu as pltpu
from jax.sharding import Mesh
from jax.sharding import PartitionSpec as P

N = 640
HALF_BAND = 64
BLK = 32
SEG = 4
SLOTS = 4
LANES = 128
KB = N // LANES
ROWS = SEG * BLK
OUT_ROWS = (2 * N + 1) * 8
NT = (((1,), (1,)), ((), ()))
VMEM = pl.BlockSpec(memory_space=pltpu.VMEM)
SMEM = pl.BlockSpec(memory_space=pltpu.SMEM)
f32 = jnp.float32
bf16 = jnp.bfloat16


def bin_order():
    return np.concatenate([np.arange(0, N, 2), np.arange(1, N, 2)])


def fourier_table():
    bins = bin_order()
    phase = (np.arange(N)[:, None] * bins[None, :]) % (2 * N)
    angle = phase * (math.pi / N)
    real = np.cos(angle).reshape(N, KB, 1, LANES)
    imag = -np.sin(angle).reshape(N, KB, 1, LANES)
    return np.concatenate([real, imag], axis=2).reshape(N, 2 * N).astype(bf16)


def window_table():
    bins = bin_order()
    return (np.abs(bins[:, None] - bins[None, :]) <= HALF_BAND).astype(bf16)


def bin_rows():
    bins = bin_order()
    counts = np.minimum(bins, HALF_BAND) + np.minimum(N - 1 - bins, HALF_BAND) + 1
    weight = np.where(bins == 0, 0.5, 1.0)
    return np.stack([1.0 / counts, weight]).astype(np.float32)


def order_kernel(slot_ref, *refs):
    pieces, blocks_ref = refs[:SEG], refs[SEG]
    place = lax.broadcasted_iota(jnp.int32, (2 * BLK, 2 * BLK), 0)
    onehot = (place == slot_ref[...]).astype(bf16)
    for s in range(SEG):
        rows = jnp.dot(onehot, pieces[s][0], preferred_element_type=f32).astype(bf16)
        blocks_ref[0, s * BLK : (s + 1) * BLK, :] = rows[:BLK]
        blocks_ref[1, s * BLK : (s + 1) * BLK, :] = rows[BLK:]


def grant(mib):
    return pltpu.CompilerParams(vmem_limit_bytes=mib * 2**20)


def order_rows(station_slot, pieces):
    return pl.pallas_call(
        order_kernel,
        out_shape=jax.ShapeDtypeStruct((2, ROWS, N), bf16),
        in_specs=[VMEM] * 5,
        out_specs=VMEM,
        compiler_params=grant(4),
        name="order_rows",
    )(station_slot, *pieces)


def whiten_rows(rows, table_ref, window_ref, bins_ref, spec_ref, hi_ref, lo_ref, store):
    for kb in range(KB):
        cols = slice(2 * kb * LANES, 2 * (kb + 1) * LANES)
        lanes = slice(kb * LANES, (kb + 1) * LANES)
        spec = jnp.dot(rows, table_ref[:, cols], preferred_element_type=f32)
        spec_ref[:, cols] = spec
        real, imag = spec[:, :LANES], spec[:, LANES:]
        power = real * real + imag * imag
        high = power.astype(bf16)
        hi_ref[:, lanes] = high
        lo_ref[:, lanes] = (power - high.astype(f32)).astype(bf16)
    total = jnp.dot(hi_ref[...], window_ref[...], preferred_element_type=f32)
    total += jnp.dot(lo_ref[...], window_ref[...], preferred_element_type=f32)
    factor = lax.rsqrt(total * bins_ref[0:1, :] + 1e-06)
    for kb in range(KB):
        scale = factor[:, kb * LANES : (kb + 1) * LANES]
        for part in range(2):
            start = (2 * kb + part) * LANES
            cols = slice(start, start + LANES)
            store(cols, (spec_ref[:, cols] * scale).astype(bf16))


def own_kernel(blocks_ref, table_ref, window_ref, bins_ref, white_ref, spec_ref, hi_ref, lo_ref):
    rows = blocks_ref[...].reshape(2 * ROWS, N)

    def store(cols, value):
        white_ref[:, cols] = value.astype(f32)

    whiten_rows(rows, table_ref, window_ref, bins_ref, spec_ref, hi_ref, lo_ref, store)


def whiten_scratch():
    return [
        pltpu.VMEM((2 * ROWS, 2 * N), f32),
        pltpu.VMEM((2 * ROWS, N), bf16),
        pltpu.VMEM((2 * ROWS, N), bf16),
    ]


def whiten_own(blocks, table, window, bins):
    return pl.pallas_call(
        own_kernel,
        out_shape=jax.ShapeDtypeStruct((2 * ROWS, 2 * N), f32),
        in_specs=[VMEM] * 4,
        out_specs=VMEM,
        scratch_shapes=whiten_scratch(),
        compiler_params=grant(12),
        name="whiten_own",
    )(blocks, table, window, bins)


def main_kernel(
    meta_ref,
    own_ref,
    mate_ref,
    far_ref,
    table_ref,
    window_ref,
    bins_ref,
    out_ref,
    white_ref,
    spec_ref,
    hi_ref,
    lo_ref,
    mid_ref,
    first_ref,
    cross_ref,
    lag_ref,
    low_ref,
    sems,
):
    owner, seg_index, count = meta_ref[9], meta_ref[10], meta_ref[8]
    mate = owner + 1 - 2 * (owner % 2)

    mate_pick, far_pick = 0, 0
    first_base, second_base = [], []
    for z in range(SLOTS):
        first, second = meta_ref[2 * z], meta_ref[2 * z + 1]
        device, half = second // 2, second % 2
        is_own, is_mate = device == owner, device == mate
        mate_pick = jnp.where(is_mate, half, mate_pick)
        far_pick = jnp.where(is_own | is_mate, far_pick, half)
        place = jnp.where(is_own, half, jnp.where(is_mate, 2, 3))
        second_base.append(place * ROWS)
        first_base.append((first % 2) * ROWS + seg_index * (BLK // SEG))

    white_ref[: 2 * ROWS, :] = own_ref[...]
    rows = jnp.concatenate([mate_ref[mate_pick], far_ref[far_pick]], axis=0)

    def store(cols, value):
        white_ref[2 * ROWS :, cols] = value.astype(f32)

    whiten_rows(rows, table_ref, window_ref, bins_ref, spec_ref, hi_ref, lo_ref, store)

    middle = table_ref[:, 2 * 2 * LANES : 2 * 3 * LANES]
    even = lax.broadcasted_iota(jnp.int32, (1, 2 * LANES), 1) % LANES < LANES // 2
    mid_ref[:, : 2 * LANES] = jnp.where(even, middle, jnp.zeros_like(middle))
    mid_ref[:, 2 * LANES :] = jnp.where(even, jnp.zeros_like(middle), middle)

    for z in range(SLOTS):
        for s in range(SEG):
            start = pl.multiple_of(first_base[z] + s * BLK, 8)
            first_ref[s * 8 : (s + 1) * 8, :] = white_ref[pl.ds(start, 8), :]

        def cross_step(kb, carry, z=z):
            real_col = pl.multiple_of(2 * kb * LANES, LANES)
            imag_col = pl.multiple_of((2 * kb + 1) * LANES, LANES)
            weight = bins_ref[1:2, pl.ds(pl.multiple_of(kb * LANES, LANES), LANES)]
            for half in range(2):
                second = []
                for s in range(SEG):
                    start = pl.multiple_of(second_base[z] + s * BLK + half * 16, 16)
                    second.append(
                        (
                            white_ref[pl.ds(start, 16), pl.ds(real_col, LANES)] * weight,
                            white_ref[pl.ds(start, 16), pl.ds(imag_col, LANES)] * weight,
                        )
                    )
                for i in range(BLK // SEG):
                    real, imag = 0.0, 0.0
                    for s in range(SEG):
                        row = slice(s * 8 + i, s * 8 + i + 1)
                        a_re = first_ref[row, pl.ds(real_col, LANES)]
                        a_im = first_ref[row, pl.ds(imag_col, LANES)]
                        b_re, b_im = second[s]
                        real = real + (a_re * b_re + a_im * b_im)
                        imag = imag + (a_im * b_re - a_re * b_im)
                    at = slice(i * BLK + half * 16, i * BLK + half * 16 + 16)
                    cross_ref[at, pl.ds(real_col, LANES)] = real.astype(bf16)
                    cross_ref[at, pl.ds(imag_col, LANES)] = imag.astype(bf16)
            return carry

        lax.fori_loop(0, KB, cross_step, 0)

        step = N // 2
        for half in range(2):
            at = slice(half * step, (half + 1) * step)
            low_side = lax.dot_general(
                table_ref[at, : 4 * LANES], cross_ref[:, : 4 * LANES], NT, preferred_element_type=f32
            ) + lax.dot_general(
                mid_ref[at, : 2 * LANES],
                cross_ref[:, 4 * LANES : 6 * LANES],
                NT,
                preferred_element_type=f32,
            )
            high_side = lax.dot_general(
                table_ref[at, 6 * LANES :], cross_ref[:, 6 * LANES :], NT, preferred_element_type=f32
            ) + lax.dot_general(
                mid_ref[at, 2 * LANES :],
                cross_ref[:, 4 * LANES : 6 * LANES],
                NT,
                preferred_element_type=f32,
            )
            minus, plus = low_side - high_side, low_side + high_side
            for ct in range(2):
                lanes = slice(ct * LANES, (ct + 1) * LANES)
                start = half * step * 8 + ct * 4 + z
                lag_ref[pl.ds(start, step, stride=8), :] = minus[:, lanes]
                lag_ref[pl.ds(start + N * 8, step, stride=8), :] = plus[:, lanes]

    slot = lax.broadcasted_iota(jnp.int32, (8, LANES), 0) % SLOTS
    scale = 2.0 / math.sqrt(2.0 * N * SEG)
    chunks = 8
    size = 2 * N * 8 // chunks
    copies = []
    for c in range(chunks):
        value = lag_ref[c * size : (c + 1) * size, :].reshape(size // 8, 8, LANES)
        value = jnp.where((slot < count)[None], value * scale, 0.0)
        low_ref[c * size : (c + 1) * size, :] = value.reshape(size, LANES).astype(bf16)
        copy = pltpu.make_async_copy(
            low_ref.at[pl.ds(c * size, size)], out_ref.at[pl.ds(c * size, size)], sems.at[c]
        )
        copy.start()
        copies.append(copy)
    last = pltpu.make_async_copy(
        low_ref.at[pl.ds(0, 8)], out_ref.at[pl.ds(2 * N * 8, 8)], sems.at[chunks]
    )
    last.start()
    for copy in copies:
        copy.wait()
    last.wait()


def correlate(meta, own_white, mate, far, table, window, bins):
    return pl.pallas_call(
        main_kernel,
        out_shape=jax.ShapeDtypeStruct((OUT_ROWS, LANES), bf16),
        in_specs=[SMEM] + [VMEM] * 6,
        out_specs=pl.BlockSpec(memory_space=pltpu.HBM),
        scratch_shapes=[pltpu.VMEM((4 * ROWS, 2 * N), f32)]
        + whiten_scratch()
        + [
            pltpu.VMEM((N, 4 * LANES), bf16),
            pltpu.VMEM((BLK, 2 * N), f32),
            pltpu.VMEM((2 * ROWS, 2 * N), bf16),
            pltpu.VMEM((2 * N * 8, LANES), f32),
            pltpu.VMEM((2 * N * 8, LANES), bf16),
            pltpu.SemaphoreType.DMA((9,)),
        ],
        compiler_params=grant(32),
        name="correlate",
    )(meta, own_white, mate, far, table, window, bins)


def unpack(packed):
    lags = 2 * N + 1
    split = packed.reshape(lags, 2, SLOTS, LANES)
    return jnp.transpose(split, (2, 0, 1, 3)).reshape(SLOTS, lags, 2 * LANES)


def body(traces, station_slot, block_pairs, pair_count):
    pair = ("chip", "core")
    owners = lax.axis_size("chip") * 2
    table = jnp.asarray(fourier_table())
    window = jnp.asarray(window_table())
    bins = jnp.asarray(bin_rows())

    def along(distance):
        return [(i, (i + distance) % SEG) for i in range(SEG)]

    pieces = [traces] + [lax.ppermute(traces, "seg", along(d)) for d in (1, 3, 2)]
    blocks = order_rows(station_slot, pieces)
    mates = [(i, i ^ 1) for i in range(owners)]
    crossing = [(i, i + 1) for i in range(1, owners - 1, 2)]
    crossing += [(b, a) for a, b in crossing]
    far = lax.ppermute(blocks, pair, crossing)
    mate = lax.ppermute(blocks, pair, mates)
    own_white = whiten_own(blocks, table, window, bins)
    place = jnp.stack([lax.axis_index(pair), lax.axis_index("seg")]).astype(jnp.int32)
    meta = jnp.concatenate([block_pairs.reshape(-1), pair_count, place])
    return unpack(correlate(meta, own_white, mate, far, table, window, bins))


def solution(mesh):
    devices = mesh.devices.reshape(SEG, -1, 2)
    split = Mesh(devices, ("seg", "chip", "core"))
    pair = ("chip", "core")
    return jax.shard_map(
        body,
        mesh=split,
        in_specs=(P("seg", pair, None), P(pair, None), P(pair, None), P(pair)),
        out_specs=P(pair, None, "seg"),
        check_vma=False,
    )
```
